32 devices in a mesh: groups: 2 (over x), tensor: 8 (over z, y), head: 2 (over core).
Axes of the slice: x: 2, y: 2, z: 4, core: 2. Of those that a mesh axis runs over, the one named last changes fastest.
Arguments:
- hidden_state: bfloat16 [64, 5120], P(('groups', 'tensor', 'head')), parts along dimension 0, may hold values from -6 to 6
- input_gain: float32 [5120], replicated, may hold values from 0.5 to 1.5
- w_qkv: bfloat16 [2, 5120, 5120], P('head', None, 'tensor'), may hold values from -0.078125 to 0.078125
- query_gain: float32 [128], replicated, may hold values from 0.1 to 1.9
- key_gain: float32 [128], replicated, may hold values from 0.1 to 1.9
- slot_of: int32 [64], P('groups'), parts along dimension 0, may hold values from 0 to 31, each once
- lengths: int32 [64], P(('groups', 'tensor')), parts along dimension 0, may hold values from 1 to 384, 6144 in all
- key_cache: bfloat16 [64, 8, 384, 128], P(('groups', 'tensor'), 'head'), parts along dimension 0, may hold values from -127 to 127
- value_cache: bfloat16 [64, 8, 384, 128], P(('groups', 'tensor'), 'head'), parts along dimension 0, may hold values from -127 to 127
- key_scale: float32 [64, 8, 3], P(('groups', 'tensor'), 'head'), parts along dimension 0, may hold values from 0.003 to 1
- value_scale: float32 [64, 8, 3], P(('groups', 'tensor'), 'head'), parts along dimension 0, may hold values from 0.01 to 0.1
- w_out: bfloat16 [2, 4096, 5120], P('head', 'tensor'), may hold values from -0.0625 to 0.0625
- middle_gain: float32 [5120], replicated, may hold values from 0.5 to 1.5
- w_gate: bfloat16 [5120, 25600], P(None, ('tensor', 'head')), may hold values from -0.078125 to 0.078125
- w_up: bfloat16 [5120, 25600], P(None, ('tensor', 'head')), may hold values from -0.078125 to 0.078125
- w_down: bfloat16 [25600, 5120], P(('tensor', 'head')), may hold values from -0.0390625 to 0.0390625
Outputs:
- layer_out: bfloat16 [64, 5120], P(('groups', 'tensor', 'head')), parts along dimension 0
- new_kv: bfloat16 [64, 2, 8, 128], P(('groups', 'tensor'), None, 'head'), parts along dimension 0
The draws below stay inside these ranges and needn't reach their ends.
There are 2 independent parts, one for each index of `groups`. The reference program is written for one: setup_inputs(seed, part) draws one part's arguments, and reference() takes and returns one part's arrays. A program takes and returns all parts, laid end to end along the dimension named above; an argument that names none is the same for every part. Nothing has to cross between parts.
Inputs may be any that keep to these rules, and one draw needn't show every extreme that they name: A permutation: request r's cache lives in slot slot_of[r]. `lengths`: the largest is exactly 384 in every draw; in each part they sum to 6144.
All inputs are finite; a program needn't handle non-finite values. No bound on the sum of `lengths` on one device may be relied on, other than what follows from the above.
Results may differ from the reference program's by a relative error of at most 0.018.
The reference program's roundings to bfloat16 on the way count: a program that leaves them out, or rounds other values in their place, can miss the bound.
Values may be sent and summed in bfloat16 or wider, within the bound.
A program may use at most 128 MiB of HBM per device.

```python
import math
import jax
import jax.numpy as jnp
import numpy as np
from jax import lax

D = 5120
HEADS = 64
KVH = 8
HD = 128
FF = 25600
CACHE_LEN = 384
GROUP = 8
REQUESTS = 32
QKV_HALF = 5120
NBLK = 3


def draw_key_scale(key, part):
    lower_end = math.log(0.003)
    upper_end = math.log(0.03)
    uniform_draw = jax.random.uniform(key, (REQUESTS, KVH, NBLK), jnp.float32)
    return jnp.exp(lower_end + uniform_draw * (upper_end - lower_end))


def levels(stream_key, shape, split, least, largest):
    factor_of, own = 1.0, jax.random.fold_in(stream_key, 6)
    for position, shards_of in split:
        draws = jnp.exp(jax.random.uniform(jax.random.fold_in(own, position), (shards_of,), jnp.float32, least / len(split), largest / len(split)))
        factor_of = factor_of * jnp.repeat(draws, shape[position] // shards_of).reshape([-1 if axis == position else 1 for axis in range(len(shape))])
    return factor_of


def split_up(number_of, total, most, lean):
    portions = [(1 << 20) // math.isqrt(rank ** lean) + 1 for rank in range(2, number_of + 1)]
    rest, given = total - most - (number_of - 1), [1] * (number_of - 1)
    while rest > 0:
        movable = [i for i in range(number_of - 1) if given[i] < most]
        pool, remaining = sum([portions[i] for i in movable]), rest
        for i in movable:
            more = min(most - given[i], max(1, remaining * portions[i] // pool), rest)
            given[i] = given[i] + more
            rest = rest - more
    return np.array([most] + given)


def uneven(key, number_of, total, most, lean):
    if number_of == 2:
        one = jax.random.randint(key, (), max(1, total - most), min(most, total - 1) + 1)
        return jnp.stack([one, total - one])
    tallies = jnp.asarray(split_up(number_of, total, most, lean), jnp.int32)
    pairs = (number_of - 1) // 2
    source_of, receiver = tallies[1:1 + 2 * pairs:2], tallies[2:2 + 2 * pairs:2]
    room = jnp.minimum(source_of - 1, most - receiver)
    shifted = jax.random.randint(jax.random.fold_in(key, 1), (pairs,), 0, 1 << 20) % (room + 1)
    tallies = tallies.at[1:1 + 2 * pairs:2].set(source_of - shifted).at[2:2 + 2 * pairs:2].set(receiver + shifted)
    return tallies[jax.random.permutation(jax.random.fold_in(key, 2), number_of)]


def gaussian(rng, dims, scale, bound, split=(), held_as=jnp.bfloat16):
    array = scale * jax.random.normal(rng, dims, jnp.float32)
    if split:
        array = array * levels(rng, dims, split, -0.22, 0.18)
    return jnp.clip(array, -bound, bound).astype(held_as)


def setup_inputs(seed: int = 0, part: int = 0) -> dict:
    key_list = jax.random.split(jax.random.key(seed), 17)
    own_keys = jax.random.split(jax.random.fold_in(key_list[16], part), 17)
    hidden_state = gaussian(own_keys[0], (REQUESTS, D), 1.0, 6.0, ((0, 16),))
    input_gain = jnp.clip(1.0 + 0.1 * jax.random.normal(key_list[1], (D,), jnp.float32), 0.5, 1.5)
    w_qkv = gaussian(key_list[2], (2, D, QKV_HALF), D ** -0.5, 0.078125, ((0, 2), (2, 8)))
    query_gain = jnp.clip(1.0 + 0.18 * jax.random.normal(key_list[3], (HD,), jnp.float32), 0.1, 1.9)
    key_gain = jnp.clip(1.0 + 0.18 * jax.random.normal(key_list[4], (HD,), jnp.float32), 0.1, 1.9)
    slot_of = jax.random.permutation(own_keys[5], REQUESTS).astype(jnp.int32)
    lengths = uneven(own_keys[6], REQUESTS, REQUESTS * CACHE_LEN // 2, CACHE_LEN, 2).astype(jnp.int32)
    key_cache = jnp.clip(jax.random.uniform(own_keys[7], (REQUESTS, KVH, CACHE_LEN, HD), jnp.float32, -127.0, 127.0) * levels(own_keys[7], (REQUESTS, KVH, CACHE_LEN, HD), ((0, 8), (1, 2)), -0.4, 0.0), -127.0, 127.0).astype(jnp.bfloat16)
    value_cache = jnp.clip(jax.random.uniform(own_keys[8], (REQUESTS, KVH, CACHE_LEN, HD), jnp.float32, -127.0, 127.0) * levels(own_keys[8], (REQUESTS, KVH, CACHE_LEN, HD), ((0, 8), (1, 2)), -0.4, 0.0), -127.0, 127.0).astype(jnp.bfloat16)
    key_scale = draw_key_scale(jax.random.fold_in(jax.random.fold_in(key_list[16], part), 71), part)
    value_scale = jnp.clip(jnp.exp(math.log(0.1) - 2.3025851 * jax.random.uniform(own_keys[10], (REQUESTS, KVH, NBLK), jnp.float32) ** levels(own_keys[10], (REQUESTS, KVH, NBLK), ((0, 8), (1, 2)), -0.2, 0.2)), 0.01, 0.1)
    w_out = gaussian(key_list[11], (2, HEADS * HD // 2, D), (HEADS * HD) ** -0.5, 0.0625, ((0, 2), (1, 8)))
    middle_gain = jnp.clip(1.0 + 0.1 * jax.random.normal(key_list[12], (D,), jnp.float32), 0.5, 1.5)
    w_gate = gaussian(key_list[13], (D, FF), D ** -0.5, 0.078125, ((1, 16),))
    w_up = gaussian(key_list[14], (D, FF), D ** -0.5, 0.078125, ((1, 16),))
    w_down = gaussian(key_list[15], (FF, D), FF ** -0.5, 0.0390625, ((0, 16),))
    return {"hidden_state": hidden_state, "input_gain": input_gain, "w_qkv": w_qkv, "query_gain": query_gain, "key_gain": key_gain, "slot_of": slot_of, "lengths": lengths, "key_cache": key_cache, "value_cache": value_cache, "key_scale": key_scale, "value_scale": value_scale, "w_out": w_out, "middle_gain": middle_gain, "w_gate": w_gate, "w_up": w_up, "w_down": w_down}


EPSILON = 1e-06
THETA = 1000000.0

def rms_scale(values, gain_vector):
    mean_square = lax.optimization_barrier(jnp.mean(values * values, axis=-1, keepdims=True))
    return values * lax.rsqrt(mean_square + EPSILON) * gain_vector

def rotate(values, positions):
    full_width = values.shape[-1]
    half_width = full_width // 2
    frequency = jnp.power(jnp.float32(THETA), -jnp.arange(half_width, dtype=jnp.float32) * 2.0 / full_width)
    angles = positions.astype(jnp.float32)[..., None] * frequency
    cosine = jnp.cos(angles)
    sine_part = jnp.sin(angles)
    lower_half = values[..., :half_width]
    upper_half = values[..., half_width:]
    return jnp.concatenate([lower_half * cosine - upper_half * sine_part, upper_half * cosine + lower_half * sine_part], axis=-1)

def attend_slot(operands):
    query_rot, key_rot, values_new, key_codes, value_codes, key_scales, value_scales, cached = operands
    block_size = key_codes.shape[1] // key_scales.shape[1]
    inverse_root = 1.0 / math.sqrt(query_rot.shape[-1])
    key_expand = jnp.repeat(key_scales, block_size, axis=1)
    value_expand = jnp.repeat(value_scales, block_size, axis=1)
    raw_scores = jnp.einsum('gih,gph->gip', query_rot.astype(jnp.float32), key_codes.astype(jnp.float32))
    positions = jnp.arange(key_codes.shape[1], dtype=jnp.int32)
    live_mask = positions < cached
    cache_scores = jnp.where(live_mask, raw_scores * key_expand[:, None, :] * inverse_root, -jnp.inf)
    own_scores = jnp.einsum('gih,gh->gi', query_rot.astype(jnp.float32), key_rot.astype(jnp.float32)) * inverse_root
    highest = jnp.maximum(lax.optimization_barrier(jnp.max(cache_scores, axis=-1)), own_scores)
    cache_exp = jnp.exp(cache_scores - highest[..., None])
    own_exp = jnp.exp(own_scores - highest)
    denominator = lax.optimization_barrier(jnp.sum(cache_exp, axis=-1)) + own_exp
    cache_weights = (cache_exp * value_expand[:, None, :] / denominator[..., None]).astype(jnp.bfloat16)
    own_weights = (own_exp / denominator).astype(jnp.bfloat16)
    mixed_sum = jnp.einsum('gip,gph->gih', cache_weights.astype(jnp.float32), value_codes.astype(jnp.float32))
    mixed_sum = mixed_sum + own_weights.astype(jnp.float32)[..., None] * values_new.astype(jnp.float32)[:, None, :]
    return mixed_sum.astype(jnp.bfloat16)

def reference(hidden_state, input_gain, w_qkv, query_gain, key_gain, slot_of, lengths, key_cache, value_cache, key_scale, value_scale, w_out, middle_gain, w_gate, w_up, w_down):
    normed_in = rms_scale(hidden_state.astype(jnp.float32), input_gain).astype(jnp.bfloat16)
    halves = [jnp.dot(normed_in, w_qkv[half_index], preferred_element_type=jnp.float32) for half_index in range(2)]
    qkv_all = jnp.stack(halves).astype(jnp.bfloat16)
    request_of = jnp.zeros((REQUESTS,), jnp.int32).at[slot_of].set(jnp.arange(REQUESTS, dtype=jnp.int32))
    by_slot = qkv_all[:, request_of]
    grouped = by_slot.reshape(2, REQUESTS, KVH // 2, GROUP + 2, HD).transpose(1, 0, 2, 3, 4).reshape(REQUESTS, KVH, GROUP + 2, HD)
    queries = grouped[:, :, :GROUP].astype(jnp.float32)
    keys_new = grouped[:, :, GROUP].astype(jnp.float32)
    values_new = grouped[:, :, GROUP + 1]
    query_rot = rotate(rms_scale(queries, query_gain), lengths[:, None, None]).astype(jnp.bfloat16)
    key_rot = rotate(rms_scale(keys_new, key_gain), lengths[:, None]).astype(jnp.bfloat16)
    new_kv = jnp.stack([key_rot, values_new], axis=1)
    attended = lax.map(attend_slot, (query_rot, key_rot, values_new, key_cache, value_cache, key_scale, value_scale, lengths))
    by_request = attended.reshape(REQUESTS, HEADS * HD)[slot_of]
    projected = jnp.dot(by_request, w_out.reshape(HEADS * HD, D), preferred_element_type=jnp.float32)
    middle = (hidden_state.astype(jnp.float32) + projected).astype(jnp.bfloat16)
    normed_mid = rms_scale(middle.astype(jnp.float32), middle_gain).astype(jnp.bfloat16)
    gate_part = jnp.dot(normed_mid, w_gate, preferred_element_type=jnp.float32)
    up_part = jnp.dot(normed_mid, w_up, preferred_element_type=jnp.float32)
    activation = (jax.nn.silu(gate_part) * up_part).astype(jnp.bfloat16)
    layer_out = (middle.astype(jnp.float32) + jnp.dot(activation, w_down, preferred_element_type=jnp.float32)).astype(jnp.bfloat16)
    return (layer_out, new_kv)
```

```python
import functools
import math

import jax
import jax.numpy as jnp
from jax import lax
from jax.experimental import pallas as pl
from jax.experimental.pallas import tpu as pltpu
from jax.sharding import PartitionSpec as P

EPSILON = 1e-06
THETA = 1000000.0


def rms_scale(values, gain_vector):
    mean_square = jnp.mean(values * values, axis=-1, keepdims=True)
    return values * lax.rsqrt(mean_square + EPSILON) * gain_vector


def rotate(values, positions):
    full_width = values.shape[-1]
    half_width = full_width // 2
    frequency = jnp.power(
        jnp.float32(THETA), -jnp.arange(half_width, dtype=jnp.float32) * 2.0 / full_width
    )
    angles = positions.astype(jnp.float32)[..., None] * frequency
    cosine = jnp.cos(angles)
    sine_part = jnp.sin(angles)
    lower_half = values[..., :half_width]
    upper_half = values[..., half_width:]
    return jnp.concatenate(
        [
            lower_half * cosine - upper_half * sine_part,
            upper_half * cosine + lower_half * sine_part,
        ],
        axis=-1,
    )


def gate_units(normed_rows, w_gate, w_up):
    gate_part = jnp.dot(normed_rows, w_gate, preferred_element_type=jnp.float32)
    up_part = jnp.dot(normed_rows, w_up, preferred_element_type=jnp.float32)
    return (jax.nn.silu(gate_part) * up_part).astype(jnp.bfloat16)


def softmax_weights(cache_scores, own_scores, value_expand):
    highest = jnp.maximum(jnp.max(cache_scores, axis=-1), own_scores)
    cache_exp = jnp.exp(cache_scores - highest[..., None])
    own_exp = jnp.exp(own_scores - highest)
    denominator = jnp.sum(cache_exp, axis=-1) + own_exp
    cache_weights = (cache_exp * value_expand[:, :, None, :] / denominator[..., None]).astype(
        jnp.bfloat16
    )
    own_weights = (own_exp / denominator).astype(jnp.bfloat16)
    return (cache_weights, own_weights)


MESH_ID = pl.DeviceIdType.MESH
VMEM_LIMIT = 66_500_000
TILE = 1280
CHUNKS = 2


def remote(src, dst, send_sem, recv_sem, tensor_index, head_index):
    return pltpu.make_async_remote_copy(
        src_ref=src,
        dst_ref=dst,
        send_sem=send_sem,
        recv_sem=recv_sem,
        device_id={"tensor": tensor_index, "head": head_index},
        device_id_type=MESH_ID,
    )


def partner(mt, k, nt):
    peer, bit = 0, 1
    while bit < nt:
        digit = lax.rem(lax.div(mt, bit), 2)
        peer = peer + bit * ((1 - digit) if k & bit else digit)
        bit *= 2
    return peer


def wrapped_iota(shape, axis, period):
    index = lax.broadcasted_iota(jnp.int32, shape, axis)
    wrapped = index
    for k in range(1, -(-shape[axis] // period)):
        wrapped = jnp.where(index >= k * period, index - k * period, wrapped)
    return wrapped


def dot_nt(lhs, rhs):
    return lax.dot_general(
        lhs, rhs, (((1,), (1,)), ((), ())), preferred_element_type=jnp.float32
    )


def dot_nn(lhs, rhs):
    return jnp.dot(lhs, rhs, preferred_element_type=jnp.float32)


def layer_kernel(
    nt, sizes,
    hid, gain_in, slots, lens, q_gain, k_gain, k_scale, v_scale, gain_mid,
    wq, keys, values, wo, wg, wu, wd,
    out, new_kv,
    hid_v, gin_v, slots_v, lens_v, qg_v, kg_v, ks_v, vs_v, gmid_v,
    kcb, vcb, wob, wgb, wub, wdb,
    gath_a, xbuf, acc, snd_b, rcv_b, att, rcv_d, kexp, vexp,
    own, swp, got, send2, recv2, mid32, gath_f, gacc, uacc,
    small_sem, kv_sem, wq_sem, wo_sem, wf_sem,
    ga_sem, b_sem, d_sem, swap_sem, rs_sem, gf_sem,
):
    rows, width, requests, per, heads, group, qchunks, chunks = sizes
    bf16, f32 = jnp.bfloat16, jnp.float32
    mt = lax.axis_index("tensor")
    mh = lax.axis_index("head")
    peers = [partner(mt, k, nt) for k in range(nt)]
    far_first = list(range(nt - 1, 0, -1))
    near_first = list(range(1, nt))
    cols = wq.shape[2]
    head_dim = qg_v.shape[1]
    depth = width // qchunks
    chunk = width // chunks
    pending = []

    barrier = pltpu.get_barrier_semaphore()
    for k in far_first:
        pl.semaphore_signal(
            barrier, inc=1, device_id={"tensor": peers[k], "head": mh}, device_id_type=MESH_ID
        )
    pl.semaphore_signal(
        barrier, inc=1, device_id={"tensor": mt, "head": 1 - mh}, device_id_type=MESH_ID
    )

    small = []
    for i, (src, dst) in enumerate(
        [
            (hid, hid_v), (gain_in, gin_v), (slots, slots_v), (lens, lens_v), (q_gain, qg_v),
            (k_gain, kg_v), (k_scale, ks_v), (v_scale, vs_v), (gain_mid, gmid_v),
        ]
    ):
        copy = pltpu.make_async_copy(src, dst, small_sem.at[i])
        copy.start()
        small.append(copy)
    wq_copies, wo_copies, wg_copies, wu_copies, wd_copies = [], [], [], [], []
    for c in range(qchunks):
        copy = pltpu.make_async_copy(
            wq.at[0, pl.ds(c * depth, depth), :],
            wdb.at[pl.ds(0, depth), pl.ds(c * cols, cols)],
            wq_sem.at[c],
        )
        copy.start()
        wq_copies.append(copy)
    key_copy = pltpu.make_async_copy(keys, kcb, kv_sem.at[0])
    key_copy.start()
    value_copy = pltpu.make_async_copy(values, vcb, kv_sem.at[1])
    value_copy.start()

    def column_copy(src, dst, c, sem):
        span = pl.ds(c * chunk, chunk)
        copy = pltpu.make_async_copy(src.at[:, span], dst.at[:, span], sem)
        copy.start()
        return copy

    for c in range(chunks):
        wo_copies.append(column_copy(wo.at[0], wob, c, wo_sem.at[c]))
    for c in range(chunks):
        wg_copies.append(column_copy(wg, wgb, c, wf_sem.at[0, c]))
        wu_copies.append(column_copy(wu, wub, c, wf_sem.at[1, c]))

    def gather_start(buf, c, sems, parts):
        send, recv, fsend, frecv = [sems.at[i, c] for i in range(4)]
        block = buf.at[c, mh, mt]
        for k in far_first:
            copy = remote(block, block, send.at[k], recv.at[mt], peers[k], mh)
            copy.start()
            pending.append(copy)
        copy = remote(block, block, fsend.at[mt], frecv.at[mt], mt, 1 - mh)
        copy.start()
        pending.append(copy)

    def gather_forward(buf, c, sems):
        send, recv, fsend, frecv = [sems.at[i, c] for i in range(4)]
        for k in near_first:
            block = buf.at[c, mh, peers[k]]
            remote(block, block, send.at[k], recv.at[peers[k]], mt, 1 - mh).wait_recv()
            copy = remote(block, block, fsend.at[peers[k]], frecv.at[peers[k]], mt, 1 - mh)
            copy.start()
            pending.append(copy)

    def gather_finish(buf, c, sems):
        send, recv, fsend, frecv = [sems.at[i, c] for i in range(4)]
        for k in range(nt):
            block = buf.at[c, 1 - mh, peers[k]]
            remote(block, block, fsend.at[peers[k]], frecv.at[peers[k]], mt, 1 - mh).wait_recv()

    def assemble(buf, c, size):
        for h in range(2):
            for t in range(nt):
                start = (h * nt + t) * rows
                xbuf[start : start + rows, c * size : (c + 1) * size] = buf[c, h, t].astype(f32)

    small[0].wait()
    small[1].wait()
    normed = rms_scale(hid_v[...].astype(f32), gin_v[...]).astype(bf16)
    for c in range(qchunks):
        gath_a[c, mh, mt] = normed[:, c * depth : (c + 1) * depth]
    pl.semaphore_wait(barrier, nt)
    for c in range(qchunks):
        gather_start(gath_a, c, ga_sem, qchunks)

    for copy in small[2:]:
        copy.wait()
    square = (requests, requests)
    one, zero = jnp.ones((), f32), jnp.zeros((), f32)
    held = jnp.where(lax.broadcasted_iota(jnp.int32, square, 0) == slots_v[...], one, zero)
    place = lax.broadcasted_iota(jnp.int32, square, 1)
    natural = place
    for h in range(2):
        for t in range(nt):
            start, there = (h * nt + t) * rows, (t * 2 + h) * rows
            inside = jnp.logical_and(place >= start, place < start + rows)
            natural = jnp.where(inside, place - start + there, natural)
    down = lax.broadcasted_iota(jnp.int32, square, 0)
    order = jnp.where(down == natural, one, zero)
    pick = dot_nn(held.astype(bf16), order.astype(bf16)).astype(bf16)
    identity = jnp.where(down == place, one, zero).astype(bf16)
    unpick = dot_nt(identity, pick).astype(bf16)

    qrows = group * per
    slot_col = wrapped_iota((qrows, 1), 0, per)
    lens_col = jnp.sum(
        jnp.where(
            lax.broadcasted_iota(jnp.int32, (qrows, per), 1) == slot_col,
            lens_v[...].astype(f32),
            0.0,
        ),
        axis=1,
        keepdims=True,
    )
    half_dim = head_dim // 2
    lane = wrapped_iota((1, head_dim), 1, half_dim).astype(f32)
    frequency = jnp.exp(lane * (-2.0 * math.log(THETA) / head_dim))
    angles = lens_col * frequency
    cosine = jnp.cos(angles)
    sine = jnp.sin(angles)
    first_half = lax.broadcasted_iota(jnp.int32, (1, head_dim), 1) < half_dim
    signed_sine = jnp.where(first_half, -sine, sine)
    inverse_root = 1.0 / math.sqrt(head_dim)
    blocks = ks_v.shape[0]
    cache_len = kcb.shape[2]
    block_size = cache_len // blocks
    for g in range(heads):
        for b in range(blocks):
            ks = jnp.zeros((qrows, 1), f32)
            vs = jnp.zeros((qrows, 1), f32)
            for s in range(per):
                ks = jnp.where(slot_col == s, ks_v[b, s : s + 1, g : g + 1], ks)
                vs = jnp.where(slot_col == s, vs_v[b, s : s + 1, g : g + 1], vs)
            span = slice(b * block_size, (b + 1) * block_size)
            kexp[g, :, span] = jnp.broadcast_to(ks, (qrows, block_size))
            vexp[g, :, span] = jnp.broadcast_to(vs, (qrows, block_size))

    for c in range(qchunks):
        gather_forward(gath_a, c, ga_sem)
    for c in range(qchunks):
        gather_finish(gath_a, c, ga_sem)
        assemble(gath_a, c, depth)
        wq_copies[c].wait()
        product = dot_nn(
            xbuf[:, c * depth : (c + 1) * depth].astype(bf16),
            wdb[0:depth, c * cols : (c + 1) * cols],
        )
        if c == 0:
            acc[...] = product
        else:
            acc[...] += product
    by_slot = dot_nn(pick, acc[...].astype(bf16)).astype(bf16).astype(f32)
    for t in range(nt):
        snd_b[t] = by_slot[t * per : (t + 1) * per, :].astype(bf16)
    for k in far_first:
        copy = remote(
            snd_b.at[peers[k]], rcv_b.at[mt], b_sem.at[0, k], b_sem.at[1, mt], peers[k], mh
        )
        copy.start()
        pending.append(copy)
    for c in range(chunks):
        wd_copies.append(column_copy(wd, wdb, c, wf_sem.at[2, c]))
    rcv_b[mt] = snd_b[mt]
    key_copy.wait()
    value_copy.wait()
    for k in near_first:
        remote(
            snd_b.at[peers[k]], rcv_b.at[peers[k]], b_sem.at[0, k], b_sem.at[1, peers[k]], mt, 1 - mh
        ).wait_recv()

    def turned(vectors, gain, cos, sin):
        scaled = rms_scale(vectors, gain)
        return (scaled * cos + pltpu.roll(scaled, half_dim, axis=1) * sin).astype(bf16)

    def piece(g, j):
        column = (g * (group + 2) + j) * head_dim
        t, offset = column // cols, column % cols
        return rcv_b[t, :, offset : offset + head_dim].astype(f32)

    def tiled(rows_of_slots):
        return jnp.concatenate([rows_of_slots] * group, axis=0)

    positions = lax.broadcasted_iota(jnp.int32, (qrows, cache_len), 1).astype(f32)
    live = positions < lens_col
    new_keys, new_values = [], []
    share = att.shape[2]
    for g in range(heads):
        query = jnp.concatenate([piece(g, i) for i in range(group)], axis=0)
        query_rot = turned(query, qg_v[...], cosine, signed_sine)
        key_rot = turned(tiled(piece(g, group)), kg_v[...], cosine, signed_sine)
        value = tiled(piece(g, group + 1))
        new_keys.append(key_rot.astype(f32))
        new_values.append(value)
        own_score = (
            jnp.sum(query_rot.astype(f32) * key_rot.astype(f32), axis=1, keepdims=True)
            * inverse_root
        )
        scores = dot_nt(query_rot, kcb[0, g])
        for s in range(1, per):
            scores = jnp.where(slot_col == s, dot_nt(query_rot, kcb[s, g]), scores)
        scores = jnp.where(live, scores * kexp[g] * inverse_root, -jnp.inf)
        top = jnp.maximum(jnp.max(scores, axis=1, keepdims=True), own_score)
        cache_exp = jnp.exp(scores - top)
        own_exp = jnp.exp(own_score - top)
        denominator = jnp.sum(cache_exp, axis=1, keepdims=True) + own_exp
        weights = (cache_exp * vexp[g] / denominator).astype(bf16).astype(f32)
        mixed = (own_exp / denominator).astype(bf16).astype(f32) * value
        for s in range(per):
            mine = jnp.where(slot_col == s, weights, 0.0).astype(bf16)
            mixed = mixed + dot_nn(mine, vcb[s, g])
        for i in range(group):
            column = (g * group + i) * head_dim
            t, offset = column // share, column % share
            att[t, :, offset : offset + head_dim] = mixed[i * per : (i + 1) * per, :].astype(bf16)
        first, last = g * group * head_dim // share, (g + 1) * group * head_dim // share
        for t in range(first, last):

            @pl.when(mt != t)
            def _():
                remote(att.at[t], rcv_d.at[mt], d_sem.at[0, t], d_sem.at[1, mt], t, mh).start()

            @pl.when(mt == t)
            def _():
                rcv_d[t] = att[t]

    for s in range(per):
        for index, parts in ((0, new_keys), (1, new_values)):
            new_kv[s, index] = jnp.concatenate([p[s : s + 1, :] for p in parts], axis=0).astype(bf16)

    for k in near_first:
        peer = peers[k]
        copy = remote(att.at[peer], rcv_d.at[peer], d_sem.at[0, peer], d_sem.at[1, peer], mt, 1 - mh)
        copy.wait_recv()
        pending.append(copy)
    by_slot = jnp.concatenate([rcv_d[t].astype(f32) for t in range(nt)], axis=0)
    attended = dot_nn(unpick, by_slot.astype(bf16)).astype(bf16)

    half_rows = requests // 2
    tiles = chunk // TILE if chunk % TILE == 0 else 1
    tile = chunk // tiles

    def partial(stage, lhs, buf, c, copy):
        copy.wait()
        for j in range(tiles):
            span = slice(c * chunk + j * tile, c * chunk + (j + 1) * tile)
            product = dot_nn(lhs, buf[:, span])
            upper, lower = product[:half_rows], product[half_rows:]
            within = slice(j * tile, (j + 1) * tile)
            own[stage, c, :, within] = jnp.where(mh == 0, upper, lower)
            swp[stage, c, :, within] = jnp.where(mh == 0, lower, upper).astype(bf16)
        swap(stage, c).start()

    def swap(stage, c):
        sems = swap_sem.at[stage, c]
        return remote(swp.at[stage, c], got.at[stage, c], sems.at[0], sems.at[1], mt, 1 - mh)

    def scatter(stage, c):
        copy = swap(stage, c)
        copy.wait_recv()
        pending.append(copy)
        both = own[stage, c] + got[stage, c].astype(f32)
        for t in range(nt):
            send2[stage, c, t] = both[t * rows : (t + 1) * rows, :].astype(bf16)
        for k in far_first:
            copy = remote(
                send2.at[stage, c, peers[k]],
                recv2.at[stage, c, mt],
                rs_sem.at[stage, 0, c, k],
                rs_sem.at[stage, 1, c, mt],
                peers[k],
                mh,
            )
            copy.start()
            pending.append(copy)

    def collect(stage, c):
        total = send2[stage, c, mt].astype(f32)
        for k in near_first:
            peer = peers[k]
            remote(
                send2.at[stage, c, peer],
                recv2.at[stage, c, peer],
                rs_sem.at[stage, 0, c, k],
                rs_sem.at[stage, 1, c, peer],
                mt,
                1 - mh,
            ).wait_recv()
            total = total + recv2[stage, c, peer].astype(f32)
        return total

    def reduce_all(stage, lhs, buf, copies):
        for c in range(chunks):
            partial(stage, lhs, buf, c, copies[c])
            if c > 0:
                scatter(stage, c - 1)
        scatter(stage, chunks - 1)

    reduce_all(0, attended, wob, wo_copies)
    for c in range(chunks):
        span = slice(c * chunk, (c + 1) * chunk)
        middle = (collect(0, c) + hid_v[:, span].astype(f32)).astype(bf16)
        gath_f[c, mh, mt] = middle
        gather_start(gath_f, c, gf_sem, chunks)
        mid32[:, span] = middle.astype(f32)

    squares = jnp.zeros((requests, 1), f32)
    gather_forward(gath_f, 0, gf_sem)
    for c in range(chunks):
        span = slice(c * chunk, (c + 1) * chunk)
        gather_finish(gath_f, c, gf_sem)
        assemble(gath_f, c, chunk)
        part = xbuf[:, span]
        squares = squares + jnp.sum(part * part, axis=1, keepdims=True)
        lhs = (part * gmid_v[:, span]).astype(bf16)
        wg_copies[c].wait()
        product = dot_nt(lhs, wgb[:, span])
        if c == 0:
            gacc[...] = product
        else:
            gacc[...] += product
        if c + 1 < chunks:
            gather_forward(gath_f, c + 1, gf_sem)
        wu_copies[c].wait()
        product = dot_nt(lhs, wub[:, span])
        if c == 0:
            uacc[...] = product
        else:
            uacc[...] += product
    row_scale = lax.rsqrt(squares / width + EPSILON)
    gate = gacc[...] * row_scale
    activation = (gate / (1.0 + jnp.exp(-gate)) * (uacc[...] * row_scale)).astype(bf16)

    reduce_all(1, activation, wdb, wd_copies)
    for c in range(chunks):
        span = slice(c * chunk, (c + 1) * chunk)
        out[:, span] = mid32[:, span] + collect(1, c)
    for copy in pending:
        copy.wait_send()


def layer(
    nt, hidden_state, input_gain, slot_of, lengths, query_gain, key_gain, key_scale, value_scale,
    middle_gain, w_qkv, key_cache, value_cache, w_out, w_gate, w_up, w_down,
):
    rows, width = hidden_state.shape
    requests = rows * nt * 2
    per = requests // nt
    cols = w_qkv.shape[2]
    share = w_out.shape[1]
    units = w_gate.shape[1]
    heads, cache_len, head_dim = key_cache.shape[1:]
    blocks = key_scale.shape[2]
    group = cols * nt // (heads * head_dim) - 2
    qchunks, chunks = 4, CHUNKS
    qrows = group * per
    chunk = width // chunks
    half_rows = requests // 2
    sizes = (rows, width, requests, per, heads, group, qchunks, chunks)
    vmem = pl.BlockSpec(memory_space=pltpu.VMEM)
    anyspace = pl.BlockSpec(memory_space=pl.ANY)
    dma = pltpu.SemaphoreType.DMA
    V, bf16, f32, i32 = pltpu.VMEM, jnp.bfloat16, jnp.float32, jnp.int32
    return pl.pallas_call(
        functools.partial(layer_kernel, nt, sizes),
        out_shape=(
            jax.ShapeDtypeStruct((rows, width), f32),
            jax.ShapeDtypeStruct((per, 2, heads, head_dim), bf16),
        ),
        in_specs=[anyspace] * 16,
        out_specs=(vmem, vmem),
        scratch_shapes=[
            V((rows, width), bf16),
            V((1, width), f32),
            V((1, requests), i32),
            V((1, per), i32),
            V((1, head_dim), f32),
            V((1, head_dim), f32),
            V((blocks, per, heads), f32),
            V((blocks, per, heads), f32),
            V((1, width), f32),
            V((per, heads, cache_len, head_dim), bf16),
            V((per, heads, cache_len, head_dim), bf16),
            V((share, width), bf16),
            V((units, width), bf16),
            V((units, width), bf16),
            V((units, width), bf16),
            V((qchunks, 2, nt, rows, width // qchunks), bf16),
            V((requests, width), f32),
            V((requests, cols), f32),
            V((nt, per, cols), bf16),
            V((nt, per, cols), bf16),
            V((nt, per, share), bf16),
            V((nt, per, share), bf16),
            V((heads, qrows, cache_len), f32),
            V((heads, qrows, cache_len), f32),
            V((2, chunks, half_rows, chunk), f32),
            V((2, chunks, half_rows, chunk), bf16),
            V((2, chunks, half_rows, chunk), bf16),
            V((2, chunks, nt, rows, chunk), bf16),
            V((2, chunks, nt, rows, chunk), bf16),
            V((rows, width), f32),
            V((chunks, 2, nt, rows, chunk), bf16),
            V((requests, units), f32),
            V((requests, units), f32),
            dma((9,)),
            dma((2,)),
            dma((qchunks,)),
            dma((chunks,)),
            dma((3, chunks)),
            dma((4, qchunks, nt)),
            dma((2, nt)),
            dma((2, nt)),
            dma((2, chunks, 2)),
            dma((2, 2, chunks, nt)),
            dma((4, chunks, nt)),
        ],
        compiler_params=pltpu.CompilerParams(
            collective_id=0, has_side_effects=True, vmem_limit_bytes=VMEM_LIMIT
        ),
    )(
        hidden_state,
        input_gain.reshape(1, -1),
        slot_of.reshape(1, -1),
        lengths.reshape(1, -1),
        query_gain.reshape(1, -1),
        key_gain.reshape(1, -1),
        key_scale.transpose(2, 0, 1),
        value_scale.transpose(2, 0, 1),
        middle_gain.reshape(1, -1),
        w_qkv,
        key_cache,
        value_cache,
        w_out,
        w_gate.T,
        w_up.T,
        w_down,
    )


def kernel_fits(nt, nh, hidden_state, w_qkv, key_cache, key_scale, w_out, w_gate):
    rows, width = hidden_state.shape
    units = w_gate.shape[1]
    cols, share = w_qkv.shape[2], w_out.shape[1]
    slots, heads, cache_len, head_dim = key_cache.shape
    weight_bytes = 2 * width * (share + 3 * units) + 4 * slots * heads * cache_len * head_dim
    requests = 2 * nt * rows
    other_bytes = requests * width * 34
    return (
        nh == 2
        and nt & (nt - 1) == 0
        and slots * nt == requests
        and slots % 2 == 0
        and head_dim == 128
        and cols % head_dim == 0
        and share % head_dim == 0
        and (cols * nt) % (heads * head_dim) == 0
        and ((cols * nt) // heads - 2 * head_dim) % share == 0
        and cache_len % (128 * key_scale.shape[2]) == 0
        and width % (4 * 128) == 0
        and width % (CHUNKS * 128) == 0
        and units % 16 == 0
        and width // 4 <= units
        and 4 * cols <= width
        and weight_bytes + other_bytes < VMEM_LIMIT
    )


def per_device(
    nt,
    nh,
    hidden_state,
    input_gain,
    w_qkv,
    query_gain,
    key_gain,
    slot_of,
    lengths,
    key_cache,
    value_cache,
    key_scale,
    value_scale,
    w_out,
    middle_gain,
    w_gate,
    w_up,
    w_down,
):
    rows_local = hidden_state.shape[0]
    requests = slot_of.shape[0]
    if kernel_fits(nt, nh, hidden_state, w_qkv, key_cache, key_scale, w_out, w_gate):
        layer_out, new_kv = layer(
            nt, hidden_state, input_gain, slot_of, lengths, query_gain, key_gain, key_scale,
            value_scale, middle_gain, w_qkv, key_cache, value_cache, w_out, w_gate, w_up, w_down,
        )
        return (layer_out.astype(jnp.bfloat16), new_kv)
    normed_in = rms_scale(hidden_state.astype(jnp.float32), input_gain).astype(jnp.bfloat16)
    qkv_weights = w_qkv[0]
    qkv_local = jnp.dot(
        lax.all_gather(normed_in, ("tensor", "head"), axis=0, tiled=True),
        qkv_weights,
        preferred_element_type=jnp.float32,
    ).astype(jnp.bfloat16)
    request_of = (
        jnp.zeros((requests,), jnp.int32).at[slot_of].set(jnp.arange(requests, dtype=jnp.int32))
    )
    qkv_slots = jnp.take(qkv_local, request_of, axis=0)
    owned_rows = lax.all_to_all(qkv_slots, "tensor", split_axis=0, concat_axis=1, tiled=True)
    slots_here = owned_rows.shape[0]
    kv_local = key_cache.shape[1]
    cache_len = key_cache.shape[2]
    head_dim = key_cache.shape[3]
    block_size = cache_len // key_scale.shape[2]
    group_size = owned_rows.shape[1] // (kv_local * head_dim) - 2
    grouped = owned_rows.reshape(slots_here, kv_local, group_size + 2, head_dim)
    queries = grouped[:, :, :group_size].astype(jnp.float32)
    keys_new = grouped[:, :, group_size].astype(jnp.float32)
    values_new = grouped[:, :, group_size + 1]
    query_rot = rotate(rms_scale(queries, query_gain), lengths[:, None, None]).astype(jnp.bfloat16)
    key_rot = rotate(rms_scale(keys_new, key_gain), lengths[:, None]).astype(jnp.bfloat16)
    new_kv = jnp.stack([key_rot, values_new], axis=1)
    inverse_root = 1.0 / math.sqrt(head_dim)
    own_scores = (
        jnp.einsum("rgih,rgh->rgi", query_rot, key_rot, preferred_element_type=jnp.float32)
        * inverse_root
    )
    value_expand = jnp.repeat(value_scale, block_size, axis=2)
    key_expand = jnp.repeat(key_scale, block_size, axis=2)
    positions = jnp.arange(cache_len, dtype=jnp.int32)
    live_mask = positions[None, None, None, :] < lengths[:, None, None, None]
    raw_scores = jnp.einsum(
        "rgih,rgph->rgip", query_rot, key_cache, preferred_element_type=jnp.float32
    )
    cache_scores = jnp.where(
        live_mask, raw_scores * key_expand[:, :, None, :] * inverse_root, -jnp.inf
    )
    cache_weights, own_weights = softmax_weights(cache_scores, own_scores, value_expand)
    mixed_sum = jnp.einsum(
        "rgip,rgph->rgih", cache_weights, value_cache, preferred_element_type=jnp.float32
    )
    mixed_sum = (
        mixed_sum
        + own_weights.astype(jnp.float32)[..., None] * values_new.astype(jnp.float32)[:, :, None, :]
    )
    attended = mixed_sum.astype(jnp.bfloat16).reshape(slots_here, kv_local * group_size * head_dim)
    returned = lax.all_to_all(attended, "tensor", split_axis=1, concat_axis=0, tiled=True)
    by_request = jnp.take(returned, slot_of, axis=0)
    out_weights = w_out[0]
    own_offset = lax.axis_index(("tensor", "head")) * rows_local
    partial_out = jnp.dot(by_request, out_weights, preferred_element_type=jnp.float32)
    own_rows = lax.dynamic_slice_in_dim(
        partial_out, own_offset, rows_local, 0
    ) + hidden_state.astype(jnp.float32)
    with_residual = lax.dynamic_update_slice_in_dim(partial_out, own_rows, own_offset, 0)
    summed = lax.psum(with_residual, ("tensor", "head"))
    middle_all = summed.astype(jnp.bfloat16)
    normed_mid = rms_scale(middle_all.astype(jnp.float32), middle_gain).astype(jnp.bfloat16)
    activation = gate_units(normed_mid, w_gate, w_up)
    middle = lax.dynamic_slice_in_dim(middle_all, own_offset, rows_local, 0)
    reduced = lax.psum_scatter(
        jnp.dot(activation, w_down, preferred_element_type=jnp.float32),
        ("tensor", "head"),
        scatter_dimension=0,
        tiled=True,
    )
    layer_out = (middle.astype(jnp.float32) + reduced).astype(jnp.bfloat16)
    return (layer_out, new_kv)


def solution(mesh):
    return jax.shard_map(
        functools.partial(per_device, mesh.shape["tensor"], mesh.shape["head"]),
        mesh=mesh,
        in_specs=(
            P(("groups", "tensor", "head"), None),
            P(),
            P("head", None, "tensor"),
            P(),
            P(),
            P("groups"),
            P(("groups", "tensor")),
            P(("groups", "tensor"), "head", None, None),
            P(("groups", "tensor"), "head", None, None),
            P(("groups", "tensor"), "head", None),
            P(("groups", "tensor"), "head", None),
            P("head", "tensor", None),
            P(),
            P(None, ("tensor", "head")),
            P(None, ("tensor", "head")),
            P(("tensor", "head"), None),
        ),
        out_specs=(
            P(("groups", "tensor", "head"), None),
            P(("groups", "tensor"), None, "head", None),
        ),
        check_vma=False,
    )
```
